512 devices in a mesh: ctx: 64 (over y, z), head: 8 (over x, core).
Axes of the slice: x: 4, y: 8, z: 8, core: 2. Of those that a mesh axis runs over, the one named last changes fastest.
Arguments:
- projected: bfloat16 [16384, 12288], P(('ctx', 'head')), may hold values from -6 to 6
- gate_logits: bfloat16 [16384, 64], P(('ctx', 'head')), as said below
- conv_weight: bfloat16 [4, 8192], P(None, 'head'), may hold values from -3 to 3
- decay_log: float32 [32], P('head'), as said below
- step_bias: float32 [32], P('head'), may hold values from -1 to 1
- norm_gain: float32 [128], replicated, may hold values from 0.1 to 1.9
Outputs:
- gated: bfloat16 [16384, 4096], P(('ctx', 'head'))
The draws below stay inside these ranges and needn't reach their ends.
Inputs may be any that keep to these rules, and one draw needn't show every extreme that they name: `decay_log`: logarithms of positive rates. `gate_logits`: logits of the step sizes and decays.
All inputs are finite; a program needn't handle non-finite values.
Results may differ from the reference program's by a relative error of at most 0.0049.
Values may be sent and summed in bfloat16 or wider, within the bound.
A program may use at most 128 MiB of HBM per device.

```python
import jax
import jax.numpy as jnp
from jax import lax

KEY_HEAD_COUNT = 16
HV = 32
DK = 128
DV = 128
CONV = 4
SPAN = 64
SEQUENCE_TOKENS = 16384
FEATS = 12288
CHANNELS = 8192


def head_rates(base_key):
    pick_key, speed_key = jax.random.split(jax.random.fold_in(base_key, 7))
    slow = jax.random.bernoulli(pick_key, 0.5, (HV,))
    spread = jax.random.uniform(speed_key, (HV,), minval=0.0, maxval=1.0)
    slow_rate = 0.2 / SEQUENCE_TOKENS * jnp.exp(spread * jnp.log(3.0))
    fast_rate = 0.02 * jnp.exp(spread * jnp.log(4.0))
    return jnp.where(slow, slow_rate, fast_rate).astype(jnp.float32)


def draw_decay_log(key, part):
    return jnp.log(head_rates(key))


def draw_gate_logits(key, part):
    decay_rates = head_rates(key)
    head_group_ratio = HV // KEY_HEAD_COUNT
    spike_count = 2
    first_key, key_second, key_third = jax.random.split(jax.random.fold_in(key, 11), 3)
    logit_values = jax.random.normal(first_key, (SEQUENCE_TOKENS, KEY_HEAD_COUNT, 2, head_group_ratio), jnp.float32)
    sample_positions = jax.random.randint(key_second, (spike_count,), 0, SEQUENCE_TOKENS)
    dropped_entries = jax.random.uniform(key_third, (spike_count,), minval=0.2, maxval=0.4)
    positions = jnp.arange(SEQUENCE_TOKENS, dtype=jnp.int32)
    hits = positions[:, None] == sample_positions[None, :]
    loss_values = jnp.sum(jnp.where(hits, -jnp.log(1.0 - dropped_entries)[None, :], 0.0), axis=1)
    spike_logit = loss_values[:, None, None] / decay_rates.reshape(KEY_HEAD_COUNT, head_group_ratio)[None, :, :]
    decay_factor = jnp.where(loss_values[:, None, None] > 0.0, spike_logit, logit_values[:, :, 1])
    joined = jnp.stack([logit_values[:, :, 0], decay_factor], axis=2)
    return joined.reshape(SEQUENCE_TOKENS, 2 * HV).astype(jnp.bfloat16)


def block_scale(own_key, shape, shards, low, top_value):
    def one(dim, blocks):
        steps = jax.random.uniform(jax.random.fold_in(jax.random.fold_in(own_key, 6), dim), (blocks,), jnp.float32, low / len(shards), top_value / len(shards))
        return jnp.repeat(jnp.exp(steps), shape[dim] // blocks).reshape((-1,) + (1,) * (len(shape) - dim - 1))

    gain = one(*shards[0])
    for cut in shards[1:]:
        gain = gain * one(*cut)
    return gain


def gaussian(own_key, dims, scale, most, pieces=(), held_as=jnp.bfloat16):
    result = scale * jax.random.normal(own_key, dims, jnp.float32)
    if pieces:
        result = result * block_scale(own_key, dims, pieces, -0.22, 0.18)
    return jnp.clip(result, -most, most).astype(held_as)


def setup_inputs(seed: int = 0) -> dict:
    key_list = jax.random.split(jax.random.key(seed), 7)
    projected = gaussian(key_list[0], (SEQUENCE_TOKENS, FEATS), 1.0, 6.0, ((0, 512),))
    gate_logits = draw_gate_logits(jax.random.fold_in(key_list[6], 71), 0)
    conv_weight = gaussian(key_list[2], (CONV, CHANNELS), CONV ** -0.5, 3.0, ((1, 8),))
    decay_log = draw_decay_log(jax.random.fold_in(key_list[6], 71), 0)
    step_bias = jnp.clip(jax.random.uniform(key_list[4], (HV,), jnp.float32, -1.0, 1.0) * block_scale(key_list[4], (HV,), ((0, 8),), -0.4, 0.0), -1.0, 1.0)
    norm_gain = jnp.clip(1.0 + 0.18 * jax.random.normal(key_list[5], (DV,), jnp.float32), 0.1, 1.9)
    return {"projected": projected, "gate_logits": gate_logits, "conv_weight": conv_weight, "decay_log": decay_log, "step_bias": step_bias, "norm_gain": norm_gain}


TOP_PRECISION = lax.Precision.HIGHEST

def l2_normed(inputs):
    return inputs * lax.rsqrt(lax.optimization_barrier(jnp.sum(inputs * inputs, axis=-1, keepdims=True)) + 1e-06)

def head_inputs(activated, logit_values, decay_log, step_bias):
    token_count = activated.shape[0]
    key_heads = activated.shape[1]
    head_group_ratio = logit_values.shape[-1]
    queries = jnp.repeat(l2_normed(activated[:, :, :DK]), head_group_ratio, axis=1)
    keys = jnp.repeat(l2_normed(activated[:, :, DK:2 * DK]), head_group_ratio, axis=1)
    values = activated[:, :, 2 * DK:].reshape(token_count, key_heads * head_group_ratio, DV)
    step_size = jax.nn.sigmoid(logit_values[:, :, 0].reshape(token_count, key_heads * head_group_ratio))
    decays = -jnp.exp(decay_log) * jax.nn.softplus(logit_values[:, :, 1].reshape(token_count, key_heads * head_group_ratio) + step_bias)
    return (queries, keys, values, step_size, decays)

def solve_block(matrix, target):
    return lax.linalg.triangular_solve(matrix, target, left_side=True, lower=True, unit_diagonal=True)

def span_terms(queries, keys, values, step_size, decays):
    block_len = queries.shape[0]
    cumulative = jnp.cumsum(decays, axis=0).T
    row_pos = lax.broadcasted_iota(jnp.int32, (block_len, block_len), 0)
    col_pos = lax.broadcasted_iota(jnp.int32, (block_len, block_len), 1)
    strict = row_pos > col_pos
    causal = row_pos >= col_pos
    log_gaps = cumulative[:, :, None] - cumulative[:, None, :]
    query_h = queries.transpose(1, 0, 2)
    key_h = keys.transpose(1, 0, 2)
    value_h = values.transpose(1, 0, 2)
    key_gram = jnp.einsum('htk,hsk->hts', key_h, key_h, precision=TOP_PRECISION)
    correlation = jnp.einsum('htk,hsk->hts', query_h, key_h, precision=TOP_PRECISION)
    step_h = step_size.T
    mixing = jnp.where(strict, step_h[:, :, None] * key_gram * jnp.exp(jnp.where(strict, log_gaps, 0.0)), 0.0)
    score_matrix = jnp.where(causal, correlation * jnp.exp(jnp.where(causal, log_gaps, 0.0)), 0.0)
    system = jnp.eye(block_len, dtype=jnp.float32) + mixing
    targets = jnp.concatenate([step_h[:, :, None] * value_h, (step_h * jnp.exp(cumulative))[:, :, None] * key_h], axis=-1)
    solved = solve_block(system, targets)
    value_width = value_h.shape[-1]
    state_delta = solved[:, :, :value_width]
    key_vectors = solved[:, :, value_width:]
    final_key_row = jnp.exp(cumulative[:, -1:] - cumulative)[:, :, None] * key_h
    key_width = key_h.shape[-1]
    transition = jnp.exp(cumulative[:, -1])[:, None, None] * jnp.eye(key_width, dtype=jnp.float32) - jnp.einsum('hsk,hsj->hkj', final_key_row, key_vectors, precision=TOP_PRECISION)
    state_increment = jnp.einsum('qoz,qox->qzx', final_key_row, state_delta, precision=TOP_PRECISION)
    decayed_query = jnp.exp(cumulative)[:, :, None] * query_h
    return (score_matrix, state_delta, key_vectors, transition, state_increment, decayed_query)

def span_outputs(score_matrix, state_delta, key_vectors, decayed_query, state_list):
    state_projection = jnp.einsum('rbz,rzp->rbp', key_vectors, state_list, precision=TOP_PRECISION)
    return jnp.einsum('rbz,rzp->rbp', decayed_query, state_list, precision=TOP_PRECISION) + jnp.einsum('icf,ifm->icm', score_matrix, state_delta - state_projection, precision=TOP_PRECISION)

def advance_state(transition, state_increment, state_list):
    return jnp.einsum('hij,hjv->hiv', transition, state_list, precision=TOP_PRECISION) + state_increment

def finish(core, gate_part, norm_gain):
    normed = core * lax.rsqrt(lax.optimization_barrier(jnp.mean(core * core, axis=-1, keepdims=True)) + 1e-06) * norm_gain
    return normed * jax.nn.silu(gate_part)

def reference(projected, gate_logits, conv_weight, decay_log, step_bias, norm_gain):
    head_group_ratio = HV // KEY_HEAD_COUNT
    channels = 2 * DK + head_group_ratio * DV
    features = channels + head_group_ratio * DV
    blocks = SEQUENCE_TOKENS // SPAN
    mixed_in = projected.reshape(blocks, SPAN, KEY_HEAD_COUNT, features)
    logits_in = gate_logits.reshape(blocks, SPAN, KEY_HEAD_COUNT, 2, head_group_ratio)
    conv_taps = conv_weight.astype(jnp.float32).reshape(CONV, KEY_HEAD_COUNT, channels)

    def advance(carry, inputs):
        state_list, edge_rows = carry
        block_in, block_logits = inputs
        conv_in = block_in[:, :, :channels].astype(jnp.float32)
        window = jnp.concatenate([edge_rows, conv_in], axis=0)
        mixed = conv_taps[0] * window[0:SPAN]
        for lag_step in range(1, CONV):
            mixed = mixed + conv_taps[lag_step] * window[lag_step:lag_step + SPAN]
        activated = jax.nn.silu(mixed)
        queries, keys, values, step_size, decays = head_inputs(activated, block_logits.astype(jnp.float32), decay_log, step_bias)
        score_matrix, state_delta, key_vectors, transition, state_increment, decayed_query = span_terms(queries, keys, values, step_size, decays)
        core = span_outputs(score_matrix, state_delta, key_vectors, decayed_query, state_list)
        core_half = lax.optimization_barrier(core.astype(jnp.bfloat16)).astype(jnp.float32)
        gate_part = block_in[:, :, channels:].reshape(SPAN, HV, DV).astype(jnp.float32)
        gated = finish(core_half.transpose(1, 0, 2), gate_part, norm_gain).astype(jnp.bfloat16)
        return ((advance_state(transition, state_increment, state_list), window[SPAN:]), gated.reshape(SPAN, HV * DV))
    start = (jnp.zeros((HV, DK, DV), jnp.float32), jnp.zeros((CONV - 1, KEY_HEAD_COUNT, channels), jnp.float32))
    unused, outputs = lax.scan(advance, start, (mixed_in, logits_in))
    return outputs.reshape(SEQUENCE_TOKENS, HV * DV)
```

```python
import jax
import jax.numpy as jnp
from jax import lax
from jax.sharding import PartitionSpec as P

KEY_HEAD_COUNT = 16
HV = 32
DK = 128
DV = 128
CONV = 4
SPAN = 64


TOP_PRECISION = lax.Precision.HIGHEST
ROW = 8


def passed_along(array, axis, by):
    length = lax.axis_size(axis)
    pairs = [(i, i + by) for i in range(length) if 0 <= i + by < length]
    return lax.ppermute(array, axis, pairs)


def l2_normed(inputs):
    return inputs * lax.rsqrt(jnp.sum(inputs * inputs, axis=-1, keepdims=True) + 1e-06)


def head_inputs(activated, logit_values, decay_log, step_bias):
    token_count = activated.shape[0]
    key_heads = activated.shape[1]
    head_group_ratio = logit_values.shape[-1]
    queries = jnp.repeat(l2_normed(activated[:, :, :DK]), head_group_ratio, axis=1)
    keys = jnp.repeat(l2_normed(activated[:, :, DK : 2 * DK]), head_group_ratio, axis=1)
    values = activated[:, :, 2 * DK :].reshape(token_count, key_heads * head_group_ratio, DV)
    step_size = jax.nn.sigmoid(
        logit_values[:, :, 0].reshape(token_count, key_heads * head_group_ratio)
    )
    decays = -jnp.exp(decay_log) * jax.nn.softplus(
        logit_values[:, :, 1].reshape(token_count, key_heads * head_group_ratio) + step_bias
    )
    return (queries, keys, values, step_size, decays)


def mm(spec, a, b):
    return jnp.einsum(spec, a, b, precision=TOP_PRECISION)


def unit_inverse(lower):
    n = lower.shape[-1]
    row = lax.broadcasted_iota(jnp.int32, (n, n), 0)
    col = lax.broadcasted_iota(jnp.int32, (n, n), 1)

    def joint(size):
        return (row // (2 * size) == col // (2 * size)) & (row // size != col // size)

    inverse = jnp.eye(n, dtype=jnp.float32) - jnp.where(joint(1), lower, 0.0)
    size = 2
    while size < n:
        cross = jnp.where(joint(size), lower, 0.0)
        inverse = inverse - mm("bij,bjk->bik", inverse, mm("bij,bjk->bik", cross, inverse))
        size *= 2
    return inverse


def span_terms(queries, keys, values, step_size, decays):
    n = queries.shape[1]
    cumulative = jnp.cumsum(decays, axis=1)
    row = lax.broadcasted_iota(jnp.int32, (n, n), 0)
    col = lax.broadcasted_iota(jnp.int32, (n, n), 1)
    gaps = jnp.exp(jnp.where(row >= col, cumulative[:, :, None] - cumulative[:, None, :], 0.0))
    both = mm("btk,bsk->bts", jnp.concatenate([keys, queries], axis=1), keys)
    mixing = jnp.where(row > col, step_size[:, :, None] * both[:, :n] * gaps, 0.0)
    score = jnp.where(row >= col, both[:, n:] * gaps, 0.0)
    grown = jnp.exp(cumulative)[:, :, None]
    step = step_size[:, :, None]
    targets = jnp.concatenate([step * grown * keys, -step * values], axis=-1)
    solved = mm("bij,bjk->bik", unit_inverse(mixing), targets)
    last = jnp.exp(cumulative[:, -1:] - cumulative)[:, :, None] * keys
    eye = (
        lax.broadcasted_iota(jnp.int32, (2 * DK, DK), 0)
        == lax.broadcasted_iota(jnp.int32, (2 * DK, DK), 1)
    ).astype(jnp.float32)
    step_map = jnp.exp(cumulative[:, -1])[:, None, None] * eye - mm("bsj,bsk->bjk", solved, last)
    reads = -mm("bts,bsj->btj", score, solved)
    return step_map, reads[:, :, :DK] + grown * queries, reads[:, :, DK:]


def compose(earlier, later):
    product = mm("...ij,...jk->...ik", earlier, later[..., :DK, :])
    return product + jnp.concatenate(
        [jnp.zeros_like(later[..., :DK, :]), later[..., DK:, :]], axis=-2
    )


def entering(total):
    heads = total.shape[0]
    count = lax.axis_size("ctx")
    rows = count // ROW
    parts = ROW // heads
    width = DV // parts
    along = [[r * ROW + z for z in range(ROW)] for r in range(rows)]
    across = [[r * ROW + z for r in range(rows)] for z in range(ROW)]
    mine = lax.axis_index("ctx") // ROW
    pieces = jnp.concatenate(
        [
            jnp.broadcast_to(total[None, :, :DK], (parts, heads, DK, DK)),
            total[:, DK:].reshape(heads, parts, width, DK).transpose(1, 0, 2, 3),
        ],
        axis=2,
    ).reshape(ROW, DK + width, DK)
    got = lax.all_to_all(pieces, "ctx", 0, 0, axis_index_groups=along, tiled=True)
    eye = (
        lax.broadcasted_iota(jnp.int32, (DK + width, DK), 0)
        == lax.broadcasted_iota(jnp.int32, (DK + width, DK), 1)
    ).astype(jnp.float32)
    prefixes = [eye, got[0]]
    for z in range(1, ROW):
        prefixes.append(compose(prefixes[-1], got[z]))
    sent = jnp.broadcast_to(prefixes[-1][None], (rows,) + prefixes[-1].shape)
    row_maps = lax.all_to_all(sent, "ctx", 0, 0, axis_index_groups=across, tiled=True)
    state = jnp.where(mine > 0, row_maps[0, DK:], 0.0)
    for r in range(1, rows - 1):
        longer = mm("ij,jk->ik", state, row_maps[r, :DK]) + row_maps[r, DK:]
        state = jnp.where(r < mine, longer, state)
    stack = jnp.stack(prefixes[:ROW])
    states = mm("vj,zjk->zvk", state, stack[:, :DK]) + stack[:, DK:]
    back = lax.all_to_all(states, "ctx", 0, 0, axis_index_groups=along, tiled=True)
    return back.reshape(parts, heads, width, DK).transpose(1, 0, 2, 3).reshape(heads, DV, DK)


def finish(core, gate_part, norm_gain):
    normed = core * lax.rsqrt(jnp.mean(core * core, axis=-1, keepdims=True) + 1e-06) * norm_gain
    return normed * jax.nn.silu(gate_part)


def body(projected, gate_logits, conv_weight, decay_log, step_bias, norm_gain):
    head_group_ratio = HV // KEY_HEAD_COUNT
    channels = 2 * DK + head_group_ratio * DV
    features = channels + head_group_ratio * DV
    arrived, logits_in = (
        lax.all_to_all(projected, "head", split_axis=1, concat_axis=0, tiled=True),
        lax.all_to_all(gate_logits, "head", split_axis=1, concat_axis=0, tiled=True),
    )
    local_keys = arrived.shape[1] // features
    arrived = arrived.reshape(arrived.shape[0], local_keys, features)
    conv_in = arrived[:, :, :channels]
    gate_part = arrived[:, :, channels:].reshape(
        arrived.shape[0], local_keys * head_group_ratio, DV
    )
    seq_len = conv_in.shape[0]
    edge_rows = passed_along(conv_in[seq_len - CONV + 1 :], "ctx", 1)
    window = jnp.concatenate([edge_rows, conv_in], axis=0).astype(jnp.float32)
    conv_taps = conv_weight.astype(jnp.float32).reshape(CONV, local_keys, channels)
    mixed = conv_taps[0] * window[0:seq_len]
    for lag_step in range(1, CONV):
        mixed = mixed + conv_taps[lag_step] * window[lag_step : lag_step + seq_len]
    activated = jax.nn.silu(mixed)
    logit_values = logits_in.astype(jnp.float32).reshape(seq_len, local_keys, 2, head_group_ratio)
    queries, keys, values, step_size, decays = head_inputs(
        activated, logit_values, decay_log, step_bias
    )
    local_heads = queries.shape[1]
    blocks = seq_len // SPAN

    def blocked(array):
        array = array.reshape((blocks, SPAN) + array.shape[1:])
        return jnp.moveaxis(array, 2, 1).reshape((blocks * local_heads, SPAN) + array.shape[3:])

    step_map, reads, adds = span_terms(
        blocked(queries), blocked(keys), blocked(values), blocked(step_size), blocked(decays)
    )
    step_map = step_map.reshape(blocks, local_heads, 2 * DK, DK)
    reads = reads.reshape(blocks, local_heads, SPAN, DK)
    adds = adds.reshape(blocks, local_heads, SPAN, DV)
    maps = [step_map[0]]
    for b in range(1, blocks):
        maps.append(compose(maps[-1], step_map[b]))
    state = entering(maps[-1])
    later = mm("bhtk,bhjk->bhtj", reads[1:], jnp.stack(maps[:-1]))
    reads = jnp.concatenate([reads[:1], later[..., :DK]])
    adds = jnp.concatenate([adds[:1], adds[1:] + later[..., DK:]])
    core = mm("bhtk,hvk->bhtv", reads, state) + adds
    core = core.transpose(0, 2, 1, 3).reshape(seq_len, local_heads, DV)
    core_half = core.astype(jnp.bfloat16)
    core_back = lax.optimization_barrier(core_half).astype(jnp.float32)
    gated = (
        finish(core_back, gate_part.astype(jnp.float32), norm_gain)
        .astype(jnp.bfloat16)
        .reshape(seq_len, local_heads * DV)
    )
    result = lax.all_to_all(gated, "head", split_axis=0, concat_axis=1, tiled=True)
    return result


def solution(mesh):
    return jax.shard_map(
        body,
        mesh=mesh,
        in_specs=(
            P(("ctx", "head"), None),
            P(("ctx", "head"), None),
            P(None, "head"),
            P("head"),
            P("head"),
            P(),
        ),
        out_specs=P(("ctx", "head"), None),
        check_vma=False,
    )
```

```python
import jax
import jax.numpy as jnp
from jax import lax
from jax.experimental import pallas as pl
from jax.experimental.pallas import tpu as pltpu
from jax.sharding import PartitionSpec as P

KEY_HEAD_COUNT = 16
HV = 32
DK = 128
DV = 128
CONV = 4
SPAN = 64


TOP_PRECISION = lax.Precision.HIGHEST
ROW = 8


def passed_along(array, axis, by):
    length = lax.axis_size(axis)
    pairs = [(i, i + by) for i in range(length) if 0 <= i + by < length]
    return lax.ppermute(array, axis, pairs)


def l2_normed(inputs):
    return inputs * lax.rsqrt(jnp.sum(inputs * inputs, axis=-1, keepdims=True) + 1e-06)


def head_inputs(activated, logit_values, decay_log, step_bias):
    token_count = activated.shape[0]
    key_heads = activated.shape[1]
    head_group_ratio = logit_values.shape[-1]
    queries = jnp.repeat(l2_normed(activated[:, :, :DK]), head_group_ratio, axis=1)
    keys = jnp.repeat(l2_normed(activated[:, :, DK : 2 * DK]), head_group_ratio, axis=1)
    values = activated[:, :, 2 * DK :].reshape(token_count, key_heads * head_group_ratio, DV)
    step_size = jax.nn.sigmoid(
        logit_values[:, :, 0].reshape(token_count, key_heads * head_group_ratio)
    )
    decays = -jnp.exp(decay_log) * jax.nn.softplus(
        logit_values[:, :, 1].reshape(token_count, key_heads * head_group_ratio) + step_bias
    )
    return (queries, keys, values, step_size, decays)


def mm(spec, a, b):
    return jnp.einsum(spec, a, b, precision=TOP_PRECISION)


def unit_inverse(lower):
    n = lower.shape[-1]
    row = lax.broadcasted_iota(jnp.int32, (n, n), 0)
    col = lax.broadcasted_iota(jnp.int32, (n, n), 1)

    def joint(size):
        return (row // (2 * size) == col // (2 * size)) & (row // size != col // size)

    inverse = jnp.eye(n, dtype=jnp.float32) - jnp.where(joint(1), lower, 0.0)
    size = 2
    while size < n:
        cross = jnp.where(joint(size), lower, 0.0)
        inverse = inverse - mm("bij,bjk->bik", inverse, mm("bij,bjk->bik", cross, inverse))
        size *= 2
    return inverse


def span_terms(queries, keys, values, step_size, decays):
    n = queries.shape[1]
    cumulative = jnp.cumsum(decays, axis=1)
    row = lax.broadcasted_iota(jnp.int32, (n, n), 0)
    col = lax.broadcasted_iota(jnp.int32, (n, n), 1)
    gaps = jnp.exp(jnp.where(row >= col, cumulative[:, :, None] - cumulative[:, None, :], 0.0))
    both = mm("btk,bsk->bts", jnp.concatenate([keys, queries], axis=1), keys)
    mixing = jnp.where(row > col, step_size[:, :, None] * both[:, :n] * gaps, 0.0)
    score = jnp.where(row >= col, both[:, n:] * gaps, 0.0)
    grown = jnp.exp(cumulative)[:, :, None]
    step = step_size[:, :, None]
    targets = jnp.concatenate([step * grown * keys, -step * values], axis=-1)
    solved = mm("bij,bjk->bik", unit_inverse(mixing), targets)
    last = jnp.exp(cumulative[:, -1:] - cumulative)[:, :, None] * keys
    eye = (
        lax.broadcasted_iota(jnp.int32, (2 * DK, DK), 0)
        == lax.broadcasted_iota(jnp.int32, (2 * DK, DK), 1)
    ).astype(jnp.float32)
    step_map = jnp.exp(cumulative[:, -1])[:, None, None] * eye - mm("bsj,bsk->bjk", solved, last)
    reads = -mm("bts,bsj->btj", score, solved)
    return step_map, reads[:, :, :DK] + grown * queries, reads[:, :, DK:]


def compose(earlier, later):
    product = mm("...ij,...jk->...ik", earlier, later[..., :DK, :])
    return product + jnp.concatenate(
        [jnp.zeros_like(later[..., :DK, :]), later[..., DK:, :]], axis=-2
    )


def nn(a, b):
    return lax.dot_general(
        a, b, (((1,), (0,)), ((), ())),
        precision=TOP_PRECISION, preferred_element_type=jnp.float32,
    )


def nt(a, b):
    return lax.dot_general(
        a, b, (((1,), (1,)), ((), ())),
        precision=TOP_PRECISION, preferred_element_type=jnp.float32,
    )


OFFSETS = (4, 3, 5, 2, 6, 1, 7)


def carry_kernel(
    pieces, maps, reads, adds, arrived, gain, out,
    got, prefix, row_total, row_maps, states, entered, core_reads, core_adds,
    send_a, recv_a, send_b, recv_b, send_c, recv_c,
):
    blocks, heads = reads.shape[:2]
    count = ROW
    mine = lax.axis_index("ctx")
    r, z = mine // count, lax.rem(mine, count)

    def in_row(k):
        return r * count + lax.rem(z + k, count)

    def in_column(k):
        return lax.rem(r + k, count) * count + z

    barrier = pltpu.get_barrier_semaphore()
    for k in range(1, count):
        for peer in (in_row(k), in_column(k)):
            pl.semaphore_signal(
                barrier, inc=1, device_id={"ctx": peer}, device_id_type=pl.DeviceIdType.MESH
            )
    pl.semaphore_wait(barrier, 2 * (count - 1))

    def send(source, target, send_sem, recv_sem, peer):
        copy = pltpu.make_async_remote_copy(
            src_ref=source, dst_ref=target, send_sem=send_sem, recv_sem=recv_sem,
            device_id={"ctx": peer}, device_id_type=pl.DeviceIdType.MESH,
        )
        copy.start()
        return copy

    first = [
        send(
            pieces.at[lax.rem(z + k, count)], got.at[z],
            send_a.at[k], recv_a.at[k], in_row(k),
        )
        for k in OFFSETS
    ]
    got[z] = pieces[z]

    def affine(i, carry):
        b, h = i // heads, lax.rem(i, heads)
        both = nt(reads[b + 1, h], maps[b, h])
        at = pl.ds(pl.multiple_of((b + 1) * SPAN, SPAN), SPAN)
        core_reads[h, at, :] = both[:, :DK]
        core_adds[h, at, :] = both[:, DK:] + adds[b + 1, h]
        return carry

    lax.fori_loop(0, (blocks - 1) * heads, affine, 0)
    for h in range(heads):
        core_reads[h, :SPAN, :] = reads[0, h]
        core_adds[h, :SPAN, :] = adds[0, h]

    for copy in first:
        copy.wait()
    prefix[1] = got[0]

    def advance(c, carry):
        product = nn(prefix[c], got[c, :DK, :])
        prefix[c + 1, :DK, :] = product[:DK]
        prefix[c + 1, DK:, :] = product[DK:] + got[c, DK:, :]
        return carry

    lax.fori_loop(1, count - 1, advance, 0)
    product = nn(prefix[count - 1], got[count - 1, :DK, :])
    row_total[:DK, :] = product[:DK]
    row_total[DK:, :] = product[DK:] + got[count - 1, DK:, :]
    second = [
        send(row_total, row_maps.at[r], send_b.at[k], recv_b.at[k], in_column(k))
        for k in OFFSETS
    ]
    row_maps[r] = row_total[...]
    for copy in second:
        copy.wait()
    state = jnp.where(r > 0, row_maps[0, DK:, :], 0.0)
    for c in range(1, count - 1):
        longer = nn(state, row_maps[c, :DK, :]) + row_maps[c, DK:, :]
        state = jnp.where(c < r, longer, state)
    states[0] = state
    for c in range(1, count):
        states[c] = nn(state, prefix[c, :DK, :]) + prefix[c, DK:, :]
    third = [
        send(
            states.at[lax.rem(z + k, count)], entered.at[z],
            send_c.at[k], recv_c.at[k], in_row(k),
        )
        for k in OFFSETS
    ]
    entered[z] = states[z]
    for copy in third:
        copy.wait()
    features = arrived.shape[1] // heads
    for h in range(heads):
        entering = jnp.concatenate([entered[h + heads * p] for p in range(count // heads)], axis=0)
        core = nt(core_reads[h], entering) + core_adds[h]
        core = core.astype(jnp.bfloat16).astype(jnp.float32)
        at = (h // 2) * 2 * features + 2 * DK + 2 * DV + (h % 2) * DV
        gate = arrived[:, at : at + DV].astype(jnp.float32)
        scale = lax.rsqrt(jnp.mean(core * core, axis=-1, keepdims=True) + 1e-06)
        normed = core * scale * gain[...]
        out[:, h * DV : (h + 1) * DV] = (normed * jax.nn.silu(gate)).astype(jnp.bfloat16)


def carried(total, maps, reads, adds, arrived, gain):
    heads = total.shape[0]
    parts = ROW // heads
    width = DV // parts
    seq_len = arrived.shape[0]
    pieces = jnp.concatenate(
        [
            jnp.broadcast_to(total[None, :, :DK], (parts, heads, DK, DK)),
            total[:, DK:].reshape(heads, parts, width, DK).transpose(1, 0, 2, 3),
        ],
        axis=2,
    ).reshape(ROW, DK + width, DK)
    piece = (ROW, DK + width, DK)
    half = (ROW, width, DK)
    full = (heads, seq_len, DK)
    vmem = pl.BlockSpec(memory_space=pltpu.VMEM)
    return pl.pallas_call(
        carry_kernel,
        out_shape=jax.ShapeDtypeStruct((seq_len, heads * DV), jnp.bfloat16),
        in_specs=[vmem] * 6,
        out_specs=vmem,
        scratch_shapes=[
            pltpu.VMEM(piece, jnp.float32),
            pltpu.VMEM(piece, jnp.float32),
            pltpu.VMEM(piece[1:], jnp.float32),
            pltpu.VMEM(piece, jnp.float32),
            pltpu.VMEM(half, jnp.float32),
            pltpu.VMEM(half, jnp.float32),
            pltpu.VMEM(full, jnp.float32),
            pltpu.VMEM(full, jnp.float32),
        ]
        + [pltpu.SemaphoreType.DMA((ROW,))] * 6,
        compiler_params=pltpu.CompilerParams(collective_id=0, has_side_effects=True),
    )(pieces, maps, reads, adds, arrived, gain)


def body(projected, gate_logits, conv_weight, decay_log, step_bias, norm_gain):
    head_group_ratio = HV // KEY_HEAD_COUNT
    channels = 2 * DK + head_group_ratio * DV
    features = channels + head_group_ratio * DV
    arrived, logits_in = (
        lax.all_to_all(projected, "head", split_axis=1, concat_axis=0, tiled=True),
        lax.all_to_all(gate_logits, "head", split_axis=1, concat_axis=0, tiled=True),
    )
    local_keys = arrived.shape[1] // features
    flat = arrived
    arrived = arrived.reshape(arrived.shape[0], local_keys, features)
    conv_in = arrived[:, :, :channels]
    seq_len = conv_in.shape[0]
    edge_rows = passed_along(conv_in[seq_len - CONV + 1 :], "ctx", 1)
    window = jnp.concatenate([edge_rows, conv_in], axis=0).astype(jnp.float32)
    conv_taps = conv_weight.astype(jnp.float32).reshape(CONV, local_keys, channels)
    mixed = conv_taps[0] * window[0:seq_len]
    for lag_step in range(1, CONV):
        mixed = mixed + conv_taps[lag_step] * window[lag_step : lag_step + seq_len]
    activated = jax.nn.silu(mixed)
    logit_values = logits_in.astype(jnp.float32).reshape(seq_len, local_keys, 2, head_group_ratio)
    queries, keys, values, step_size, decays = head_inputs(
        activated, logit_values, decay_log, step_bias
    )
    local_heads = queries.shape[1]
    blocks = seq_len // SPAN

    def blocked(array):
        array = array.reshape((blocks, SPAN) + array.shape[1:])
        return jnp.moveaxis(array, 2, 1).reshape((blocks * local_heads, SPAN) + array.shape[3:])

    step_map, reads, adds = span_terms(
        blocked(queries), blocked(keys), blocked(values), blocked(step_size), blocked(decays)
    )
    step_map = step_map.reshape(blocks, local_heads, 2 * DK, DK)
    reads = reads.reshape(blocks, local_heads, SPAN, DK)
    adds = adds.reshape(blocks, local_heads, SPAN, DV)
    maps = [step_map[0]]
    for b in range(1, blocks):
        maps.append(compose(maps[-1], step_map[b]))
    gated = carried(
        maps[-1], jnp.stack(maps[:-1]), reads, adds, flat, norm_gain.reshape(1, DV)
    )
    result = lax.all_to_all(gated, "head", split_axis=0, concat_axis=1, tiled=True)
    return result


def solution(mesh):
    return jax.shard_map(
        body,
        mesh=mesh,
        in_specs=(
            P(("ctx", "head"), None),
            P(("ctx", "head"), None),
            P(None, "head"),
            P("head"),
            P("head"),
            P(),
        ),
        out_specs=P(("ctx", "head"), None),
        check_vma=False,
    )
```

```python
import jax
import jax.numpy as jnp
from jax import lax
from jax.experimental import pallas as pl
from jax.experimental.pallas import tpu as pltpu
from jax.sharding import PartitionSpec as P

KEY_HEAD_COUNT = 16
HV = 32
DK = 128
DV = 128
CONV = 4
SPAN = 64


TOP_PRECISION = lax.Precision.HIGHEST
ROW = 8


def passed_along(array, axis, by):
    length = lax.axis_size(axis)
    pairs = [(i, i + by) for i in range(length) if 0 <= i + by < length]
    return lax.ppermute(array, axis, pairs)


def nn(a, b):
    return lax.dot_general(
        a, b, (((1,), (0,)), ((), ())),
        precision=TOP_PRECISION, preferred_element_type=jnp.float32,
    )


def nt(a, b):
    return lax.dot_general(
        a, b, (((1,), (1,)), ((), ())),
        precision=TOP_PRECISION, preferred_element_type=jnp.float32,
    )


def tn(a, b):
    return lax.dot_general(
        a, b, (((0,), (0,)), ((), ())),
        precision=TOP_PRECISION, preferred_element_type=jnp.float32,
    )


def iotas(rows, cols):
    return (
        lax.broadcasted_iota(jnp.int32, (rows, cols), 0),
        lax.broadcasted_iota(jnp.int32, (rows, cols), 1),
    )


def unit_inverses(lowers):
    n = lowers[0].shape[0]
    row, col = iotas(n, n)

    def joint(size):
        return (row // (2 * size) == col // (2 * size)) & (row // size != col // size)

    eye = (row == col).astype(jnp.float32)
    inverses = [eye - jnp.where(joint(1), low, 0.0) for low in lowers]
    size = 2
    while size < n:
        here = joint(size)
        inner = [nn(jnp.where(here, low, 0.0), inv) for low, inv in zip(lowers, inverses)]
        inverses = [inv - nn(inv, part) for inv, part in zip(inverses, inner)]
        size *= 2
    return inverses


def terms_kernel(
    arrived, edge, taps, columns, rows, pieces, maps, reads, adds, window, active, total
):
    blocks, heads = reads.shape[:2]
    ratio = HV // KEY_HEAD_COUNT
    key_heads = heads // ratio
    channels = (2 + ratio) * DK
    features = channels + ratio * DV
    seq_len = arrived.shape[0]
    pad = edge.shape[0]
    window[:pad, :] = edge[...].astype(jnp.float32)
    for j in range(key_heads):
        window[pad:, j * channels : (j + 1) * channels] = arrived[
            :, j * features : j * features + channels
        ].astype(jnp.float32)
    for b in range(blocks):
        for g in range(key_heads * channels // DK):
            at = slice(g * DK, (g + 1) * DK)
            low = b * SPAN + pad - CONV + 1
            mixed = taps[0:1, at] * window[low : low + SPAN, at]
            for i in range(1, CONV):
                mixed = mixed + taps[i : i + 1, at] * window[low + i : low + i + SPAN, at]
            mixed = jax.nn.silu(mixed)
            if g % (2 + ratio) < 2:
                mixed = mixed * lax.rsqrt(jnp.sum(mixed * mixed, axis=-1, keepdims=True) + 1e-06)
            active[b * SPAN : (b + 1) * SPAN, at] = mixed
    row, col = iotas(SPAN, SPAN)
    wide_row, wide_col = iotas(2 * DK, DK)
    eye = (wide_row == wide_col).astype(jnp.float32)
    for h in range(heads):
        total[h] = eye
    per = 2

    def block_terms(step, carry):
        items = [(step * per + p, h) for p in range(per) for h in range(heads)]
        keys, queries, values, both = [], [], [], []
        for p in range(per):
            at = pl.ds(pl.multiple_of((step * per + p) * SPAN, SPAN), SPAN)
            for j in range(key_heads):
                base = j * channels
                query = active[at, base : base + DK]
                key = active[at, base + DK : base + 2 * DK]
                product = nt(jnp.concatenate([key, query], axis=0), key)
                for i in range(ratio):
                    first = base + 2 * DK + i * DV
                    values.append(active[at, first : first + DV])
                    keys.append(key)
                    queries.append(query)
                    both.append(product)
        sums, steps, gaps, mixing = [], [], [], []
        for n, (b, h) in enumerate(items):
            pair = columns[b, h]
            sums.append(pair[:, 0:1])
            steps.append(pair[:, 1:2])
            gaps.append(jnp.exp(jnp.where(row >= col, sums[n] - rows[b, h], 0.0)))
            mixing.append(jnp.where(row > col, steps[n] * both[n][:SPAN] * gaps[n], 0.0))
        inverses = unit_inverses(mixing)
        solved = []
        for n in range(len(items)):
            grown = jnp.exp(sums[n])
            target = jnp.concatenate([steps[n] * grown * keys[n], -steps[n] * values[n]], axis=1)
            solved.append(nn(inverses[n], target))
        for n, (b, h) in enumerate(items):
            end = rows[b, h][:, SPAN - 1 : SPAN]
            last = jnp.exp(end - sums[n]) * keys[n]
            change = jnp.exp(end) * eye - tn(solved[n], last)
            score = jnp.where(row >= col, both[n][SPAN:] * gaps[n], 0.0)
            read = nn(score, solved[n])
            reads[b, h] = jnp.exp(sums[n]) * queries[n] - read[:, :DK]
            adds[b, h] = -read[:, DK:]
            product = nn(total[h], change[:DK])
            total[h, :DK, :] = product[:DK]
            total[h, DK:, :] = product[DK:] + change[DK:]
            maps[b, h] = total[h]
        return carry

    lax.fori_loop(0, blocks // per, block_terms, 0)
    width = pieces.shape[1] - DK
    for piece in range(ROW):
        h, part = piece % heads, piece // heads
        pieces[piece, :DK, :] = total[h, :DK, :]
        pieces[piece, DK:, :] = total[h, DK + part * width : DK + (part + 1) * width, :]


def local_terms(arrived, edge, taps, columns, rows):
    blocks, heads = columns.shape[:2]
    seq_len = arrived.shape[0]
    width = DV * heads // ROW
    channels = taps.shape[1]
    vmem = pl.BlockSpec(memory_space=pltpu.VMEM)
    return pl.pallas_call(
        terms_kernel,
        out_shape=[
            jax.ShapeDtypeStruct((ROW, DK + width, DK), jnp.float32),
            jax.ShapeDtypeStruct((blocks, heads, 2 * DK, DK), jnp.float32),
            jax.ShapeDtypeStruct((blocks, heads, SPAN, DK), jnp.float32),
            jax.ShapeDtypeStruct((blocks, heads, SPAN, DV), jnp.float32),
        ],
        in_specs=[vmem] * 5,
        out_specs=[vmem] * 4,
        scratch_shapes=[
            pltpu.VMEM((seq_len + edge.shape[0], channels), jnp.float32),
            pltpu.VMEM((seq_len, channels), jnp.float32),
            pltpu.VMEM((heads, 2 * DK, DK), jnp.float32),
        ],
    )(arrived, edge, taps, columns, rows)


OFFSETS = (4, 3, 5, 2, 6, 1, 7)


def carry_kernel(
    pieces, maps, reads, adds, arrived, gain, out,
    got, prefix, row_total, row_maps, states, entered, core_reads, core_adds, gated, landed,
    send_a, recv_a, send_b, recv_b, send_c, recv_c, send_d, recv_d,
):
    blocks, heads = reads.shape[:2]
    count = ROW
    mine = lax.axis_index("ctx")
    r, z = mine // count, lax.rem(mine, count)

    def in_row(k):
        return r * count + lax.rem(z + k, count)

    def in_column(k):
        return lax.rem(r + k, count) * count + z

    barrier = pltpu.get_barrier_semaphore()
    for k in range(1, count):
        for peer in (in_row(k), in_column(k)):
            pl.semaphore_signal(
                barrier, inc=1, device_id={"ctx": peer}, device_id_type=pl.DeviceIdType.MESH
            )
    groups = lax.axis_size("head")
    group = lax.axis_index("head")
    for k in range(1, groups):
        pl.semaphore_signal(
            barrier, inc=1, device_id={"head": lax.rem(group + k, groups)},
            device_id_type=pl.DeviceIdType.MESH,
        )
    pl.semaphore_wait(barrier, 2 * (count - 1) + groups - 1)

    def send(source, target, send_sem, recv_sem, peer, axis="ctx"):
        copy = pltpu.make_async_remote_copy(
            src_ref=source, dst_ref=target, send_sem=send_sem, recv_sem=recv_sem,
            device_id={axis: peer}, device_id_type=pl.DeviceIdType.MESH,
        )
        copy.start()
        return copy

    first = [
        send(
            pieces.at[lax.rem(z + k, count)], got.at[z],
            send_a.at[k], recv_a.at[k], in_row(k),
        )
        for k in OFFSETS
    ]
    got[z] = pieces[z]

    def affine(i, carry):
        b, h = i // heads, lax.rem(i, heads)
        both = nt(reads[b + 1, h], maps[b, h])
        at = pl.ds(pl.multiple_of((b + 1) * SPAN, SPAN), SPAN)
        core_reads[h, at, :] = both[:, :DK]
        core_adds[h, at, :] = both[:, DK:] + adds[b + 1, h]
        return carry

    lax.fori_loop(0, (blocks - 1) * heads, affine, 0)
    for h in range(heads):
        core_reads[h, :SPAN, :] = reads[0, h]
        core_adds[h, :SPAN, :] = adds[0, h]

    for copy in first:
        copy.wait()
    prefix[1] = got[0]

    def advance(c, carry):
        product = nn(prefix[c], got[c, :DK, :])
        prefix[c + 1, :DK, :] = product[:DK]
        prefix[c + 1, DK:, :] = product[DK:] + got[c, DK:, :]
        return carry

    lax.fori_loop(1, count - 1, advance, 0)
    product = nn(prefix[count - 1], got[count - 1, :DK, :])
    row_total[:DK, :] = product[:DK]
    row_total[DK:, :] = product[DK:] + got[count - 1, DK:, :]
    second = [
        send(row_total, row_maps.at[r], send_b.at[k], recv_b.at[k], in_column(k))
        for k in OFFSETS
    ]
    row_maps[r] = row_total[...]
    for copy in second:
        copy.wait()
    state = jnp.where(r > 0, row_maps[0, DK:, :], 0.0)
    for c in range(1, count - 1):
        longer = nn(state, row_maps[c, :DK, :]) + row_maps[c, DK:, :]
        state = jnp.where(c < r, longer, state)
    states[0] = state
    for c in range(1, count):
        states[c] = nn(state, prefix[c, :DK, :]) + prefix[c, DK:, :]
    third = [
        send(
            states.at[lax.rem(z + k, count)], entered.at[z],
            send_c.at[k], recv_c.at[k], in_row(k),
        )
        for k in OFFSETS
    ]
    entered[z] = states[z]
    for copy in third:
        copy.wait()
    features = arrived.shape[1] // heads
    for h in range(heads):
        entering = jnp.concatenate([entered[h + heads * p] for p in range(count // heads)], axis=0)
        core = nt(core_reads[h], entering) + core_adds[h]
        core = core.astype(jnp.bfloat16).astype(jnp.float32)
        at = (h // 2) * 2 * features + 2 * DK + 2 * DV + (h % 2) * DV
        gate = arrived[:, at : at + DV].astype(jnp.float32)
        scale = lax.rsqrt(jnp.mean(core * core, axis=-1, keepdims=True) + 1e-06)
        normed = core * scale * gain[...]
        gated[:, h * DV : (h + 1) * DV] = (normed * jax.nn.silu(gate)).astype(jnp.bfloat16)
    kept = out.shape[0]

    def tokens_of(owner):
        return gated.at[pl.ds(pl.multiple_of(owner * kept, kept), kept), :]

    fourth = []
    for k in range(1, groups):
        peer = lax.rem(group + k, groups)
        fourth.append(
            send(tokens_of(peer), landed.at[group], send_d.at[k], recv_d.at[k], peer, "head")
        )
    landed[group] = tokens_of(group)[...]
    for copy in fourth:
        copy.wait()
    for g in range(groups):
        out[:, g * heads * DV : (g + 1) * heads * DV] = landed[g]


def carried(pieces, maps, reads, adds, arrived, gain):
    blocks, heads = reads.shape[:2]
    seq_len = arrived.shape[0]
    groups = lax.axis_size("head")
    width = pieces.shape[1] - DK
    piece = (ROW, DK + width, DK)
    half = (ROW, width, DK)
    full = (heads, seq_len, DK)
    vmem = pl.BlockSpec(memory_space=pltpu.VMEM)
    return pl.pallas_call(
        carry_kernel,
        out_shape=jax.ShapeDtypeStruct((seq_len // groups, groups * heads * DV), jnp.bfloat16),
        in_specs=[vmem] * 6,
        out_specs=vmem,
        scratch_shapes=[
            pltpu.VMEM(piece, jnp.float32),
            pltpu.VMEM(piece, jnp.float32),
            pltpu.VMEM(piece[1:], jnp.float32),
            pltpu.VMEM(piece, jnp.float32),
            pltpu.VMEM(half, jnp.float32),
            pltpu.VMEM(half, jnp.float32),
            pltpu.VMEM(full, jnp.float32),
            pltpu.VMEM(full, jnp.float32),
            pltpu.VMEM((seq_len, heads * DV), jnp.bfloat16),
            pltpu.VMEM((groups, seq_len // groups, heads * DV), jnp.bfloat16),
        ]
        + [pltpu.SemaphoreType.DMA((ROW,))] * 6
        + [pltpu.SemaphoreType.DMA((groups,))] * 2,
        compiler_params=pltpu.CompilerParams(collective_id=0, has_side_effects=True),
    )(pieces, maps, reads, adds, arrived, gain)


def body(projected, gate_logits, conv_weight, decay_log, step_bias, norm_gain):
    ratio = HV // KEY_HEAD_COUNT
    channels = (2 + ratio) * DK
    features = channels + ratio * DV
    logits = lax.all_to_all(gate_logits, "head", split_axis=1, concat_axis=0, tiled=True)
    arrived = lax.all_to_all(projected, "head", split_axis=1, concat_axis=0, tiled=True)
    seq_len = arrived.shape[0]
    local_keys = arrived.shape[1] // features
    heads = local_keys * ratio
    blocks = seq_len // SPAN
    logits = logits.astype(jnp.float32).reshape(seq_len, local_keys, 2, ratio)
    step_size = jax.nn.sigmoid(logits[:, :, 0].reshape(seq_len, heads))
    decays = -jnp.exp(decay_log) * jax.nn.softplus(
        logits[:, :, 1].reshape(seq_len, heads) + step_bias
    )
    sums = jnp.cumsum(decays.reshape(blocks, SPAN, heads), axis=1).transpose(0, 2, 1)
    steps = step_size.reshape(blocks, SPAN, heads).transpose(0, 2, 1)
    columns = jnp.stack([sums, steps], axis=-1)
    tail = arrived[seq_len - CONV + 1 :].reshape(CONV - 1, local_keys, features)[:, :, :channels]
    edge = passed_along(tail.reshape(CONV - 1, local_keys * channels), "ctx", 1)
    edge = jnp.concatenate([jnp.zeros((8 - CONV + 1, edge.shape[1]), edge.dtype), edge])
    pieces, maps, reads, adds = local_terms(
        arrived, edge, conv_weight.astype(jnp.float32), columns, sums[:, :, None, :]
    )
    return carried(pieces, maps, reads, adds, arrived, norm_gain.reshape(1, DV))


def solution(mesh):
    return jax.shard_map(
        body,
        mesh=mesh,
        in_specs=(
            P(("ctx", "head"), None),
            P(("ctx", "head"), None),
            P(None, "head"),
            P("head"),
            P("head"),
            P(),
        ),
        out_specs=P(("ctx", "head"), None),
        check_vma=False,
    )
```

```python
import jax
import jax.numpy as jnp
from jax import lax
from jax.experimental import pallas as pl
from jax.experimental.pallas import tpu as pltpu
from jax.sharding import PartitionSpec as P

KEY_HEAD_COUNT = 16
HV = 32
DK = 128
DV = 128
CONV = 4
SPAN = 64


TOP_PRECISION = lax.Precision.HIGHEST
ROW = 8


def passed_along(array, axis, by):
    length = lax.axis_size(axis)
    pairs = [(i, i + by) for i in range(length) if 0 <= i + by < length]
    return lax.ppermute(array, axis, pairs)


def nn(a, b):
    return lax.dot_general(
        a, b, (((1,), (0,)), ((), ())),
        precision=TOP_PRECISION, preferred_element_type=jnp.float32,
    )


def nt(a, b):
    return lax.dot_general(
        a, b, (((1,), (1,)), ((), ())),
        precision=TOP_PRECISION, preferred_element_type=jnp.float32,
    )


def tn(a, b):
    return lax.dot_general(
        a, b, (((0,), (0,)), ((), ())),
        precision=TOP_PRECISION, preferred_element_type=jnp.float32,
    )


def iotas(rows, cols):
    return (
        lax.broadcasted_iota(jnp.int32, (rows, cols), 0),
        lax.broadcasted_iota(jnp.int32, (rows, cols), 1),
    )


def unit_inverses(lowers):
    n = lowers[0].shape[0]
    row, col = iotas(n, n)

    def joint(size):
        return (row // (2 * size) == col // (2 * size)) & (row // size != col // size)

    eye = (row == col).astype(jnp.float32)
    inverses = [eye - jnp.where(joint(1), low, 0.0) for low in lowers]
    size = 2
    while size < n:
        here = joint(size)
        inner = [nn(jnp.where(here, low, 0.0), inv) for low, inv in zip(lowers, inverses)]
        inverses = [inv - nn(inv, part) for inv, part in zip(inverses, inner)]
        size *= 2
    return inverses


def terms_kernel(
    arrived, edge, taps, columns, rows, pieces, maps, reads, adds, window, active, total
):
    blocks, heads = reads.shape[:2]
    ratio = HV // KEY_HEAD_COUNT
    key_heads = heads // ratio
    channels = (2 + ratio) * DK
    features = channels + ratio * DV
    seq_len = arrived.shape[0]
    pad = edge.shape[0]
    window[:pad, :] = edge[...].astype(jnp.float32)
    for j in range(key_heads):
        window[pad:, j * channels : (j + 1) * channels] = arrived[
            :, j * features : j * features + channels
        ].astype(jnp.float32)
    for b in range(blocks):
        for g in range(key_heads * channels // DK):
            at = slice(g * DK, (g + 1) * DK)
            low = b * SPAN + pad - CONV + 1
            mixed = taps[0:1, at] * window[low : low + SPAN, at]
            for i in range(1, CONV):
                mixed = mixed + taps[i : i + 1, at] * window[low + i : low + i + SPAN, at]
            mixed = jax.nn.silu(mixed)
            if g % (2 + ratio) < 2:
                mixed = mixed * lax.rsqrt(jnp.sum(mixed * mixed, axis=-1, keepdims=True) + 1e-06)
            active[b * SPAN : (b + 1) * SPAN, at] = mixed
    row, col = iotas(SPAN, SPAN)
    wide_row, wide_col = iotas(2 * DK, DK)
    eye = (wide_row == wide_col).astype(jnp.float32)
    for h in range(heads):
        total[h] = eye
    per = 4

    def block_terms(step, carry):
        items = [(step * per + p, h) for p in range(per) for h in range(heads)]
        keys, queries, values, both = [], [], [], []
        for p in range(per):
            at = pl.ds(pl.multiple_of((step * per + p) * SPAN, SPAN), SPAN)
            for j in range(key_heads):
                base = j * channels
                query = active[at, base : base + DK]
                key = active[at, base + DK : base + 2 * DK]
                product = nt(jnp.concatenate([key, query], axis=0), key)
                for i in range(ratio):
                    first = base + 2 * DK + i * DV
                    values.append(active[at, first : first + DV])
                    keys.append(key)
                    queries.append(query)
                    both.append(product)
        sums, steps, gaps, mixing = [], [], [], []
        for n, (b, h) in enumerate(items):
            pair = columns[b, h]
            sums.append(pair[:, 0:1])
            steps.append(pair[:, 1:2])
            gaps.append(jnp.exp(jnp.where(row >= col, sums[n] - rows[b, h], 0.0)))
            mixing.append(jnp.where(row > col, steps[n] * both[n][:SPAN] * gaps[n], 0.0))
        inverses = unit_inverses(mixing)
        solved = []
        for n in range(len(items)):
            grown = jnp.exp(sums[n])
            target = jnp.concatenate([steps[n] * grown * keys[n], -steps[n] * values[n]], axis=1)
            solved.append(nn(inverses[n], target))
        for n, (b, h) in enumerate(items):
            end = rows[b, h][:, SPAN - 1 : SPAN]
            last = jnp.exp(end - sums[n]) * keys[n]
            change = jnp.exp(end) * eye - tn(solved[n], last)
            score = jnp.where(row >= col, both[n][SPAN:] * gaps[n], 0.0)
            read = nn(score, solved[n])
            reads[b, h] = jnp.exp(sums[n]) * queries[n] - read[:, :DK]
            adds[b, h] = -read[:, DK:]
            product = nn(total[h], change[:DK])
            total[h, :DK, :] = product[:DK]
            total[h, DK:, :] = product[DK:] + change[DK:]
            maps[b, h] = total[h]
        return carry

    lax.fori_loop(0, blocks // per, block_terms, 0)
    width = pieces.shape[1] - DK
    for piece in range(ROW):
        h, part = piece % heads, piece // heads
        pieces[piece, :DK, :] = total[h, :DK, :]
        pieces[piece, DK:, :] = total[h, DK + part * width : DK + (part + 1) * width, :]


def local_terms(arrived, edge, taps, columns, rows):
    blocks, heads = columns.shape[:2]
    seq_len = arrived.shape[0]
    width = DV * heads // ROW
    channels = taps.shape[1]
    vmem = pl.BlockSpec(memory_space=pltpu.VMEM)
    return pl.pallas_call(
        terms_kernel,
        out_shape=[
            jax.ShapeDtypeStruct((ROW, DK + width, DK), jnp.float32),
            jax.ShapeDtypeStruct((blocks, heads, 2 * DK, DK), jnp.float32),
            jax.ShapeDtypeStruct((blocks, heads, SPAN, DK), jnp.float32),
            jax.ShapeDtypeStruct((blocks, heads, SPAN, DV), jnp.float32),
        ],
        in_specs=[vmem] * 5,
        out_specs=[vmem] * 4,
        scratch_shapes=[
            pltpu.VMEM((seq_len + edge.shape[0], channels), jnp.float32),
            pltpu.VMEM((seq_len, channels), jnp.float32),
            pltpu.VMEM((heads, 2 * DK, DK), jnp.float32),
        ],
    )(arrived, edge, taps, columns, rows)


OFFSETS = (4, 3, 5, 2, 6, 1, 7)


def carry_kernel(
    pieces, maps, reads, adds, arrived, gain, out,
    got, prefix, row_total, row_maps, states, entered, core_reads, core_adds, gated, landed,
    send_a, recv_a, send_b, recv_b, send_c, recv_c, send_d, recv_d,
):
    blocks, heads = reads.shape[:2]
    count = ROW
    mine = lax.axis_index("ctx")
    r, z = mine // count, lax.rem(mine, count)

    def in_row(k):
        return r * count + lax.rem(z + k, count)

    def in_column(k):
        return lax.rem(r + k, count) * count + z

    barrier = pltpu.get_barrier_semaphore()
    for k in range(1, count):
        for peer in (in_row(k), in_column(k)):
            pl.semaphore_signal(
                barrier, inc=1, device_id={"ctx": peer}, device_id_type=pl.DeviceIdType.MESH
            )
    groups = lax.axis_size("head")
    group = lax.axis_index("head")
    for k in range(1, groups):
        pl.semaphore_signal(
            barrier, inc=1, device_id={"head": lax.rem(group + k, groups)},
            device_id_type=pl.DeviceIdType.MESH,
        )
    pl.semaphore_wait(barrier, 2 * (count - 1) + groups - 1)

    def send(source, target, send_sem, recv_sem, peer, axis="ctx"):
        copy = pltpu.make_async_remote_copy(
            src_ref=source, dst_ref=target, send_sem=send_sem, recv_sem=recv_sem,
            device_id={axis: peer}, device_id_type=pl.DeviceIdType.MESH,
        )
        copy.start()
        return copy

    first = [
        send(
            pieces.at[lax.rem(z + k, count)], got.at[z],
            send_a.at[k], recv_a.at[k], in_row(k),
        )
        for k in OFFSETS
    ]
    got[z] = pieces[z]

    def affine(i, carry):
        b, h = i // heads, lax.rem(i, heads)
        both = nt(reads[b + 1, h], maps[b, h])
        at = pl.ds(pl.multiple_of((b + 1) * SPAN, SPAN), SPAN)
        core_reads[h, at, :] = both[:, :DK]
        core_adds[h, at, :] = both[:, DK:] + adds[b + 1, h]
        return carry

    lax.fori_loop(0, (blocks - 1) * heads, affine, 0)
    for h in range(heads):
        core_reads[h, :SPAN, :] = reads[0, h]
        core_adds[h, :SPAN, :] = adds[0, h]

    for copy in first:
        copy.wait()
    prefix[1] = got[0]

    def advance(c, carry):
        product = nn(prefix[c], got[c, :DK, :])
        prefix[c + 1, :DK, :] = product[:DK]
        prefix[c + 1, DK:, :] = product[DK:] + got[c, DK:, :]
        return carry

    lax.fori_loop(1, count - 1, advance, 0)
    product = nn(prefix[count - 1], got[count - 1, :DK, :])
    row_total[:DK, :] = product[:DK]
    row_total[DK:, :] = product[DK:] + got[count - 1, DK:, :]
    second = [
        send(row_total, row_maps.at[r], send_b.at[k], recv_b.at[k], in_column(k))
        for k in OFFSETS
    ]
    row_maps[r] = row_total[...]
    for copy in second:
        copy.wait()
    state = jnp.where(r > 0, row_maps[0, DK:, :], 0.0)
    for c in range(1, count - 1):
        longer = nn(state, row_maps[c, :DK, :]) + row_maps[c, DK:, :]
        state = jnp.where(c < r, longer, state)
    states[0] = state
    for c in range(1, count):
        states[c] = nn(state, prefix[c, :DK, :]) + prefix[c, DK:, :]
    third = [
        send(
            states.at[lax.rem(z + k, count)], entered.at[z],
            send_c.at[k], recv_c.at[k], in_row(k),
        )
        for k in OFFSETS
    ]
    entered[z] = states[z]
    for copy in third:
        copy.wait()
    features = arrived.shape[1] // heads
    for h in range(heads):
        entering = jnp.concatenate([entered[h + heads * p] for p in range(count // heads)], axis=0)
        core = nt(core_reads[h], entering) + core_adds[h]
        core = core.astype(jnp.bfloat16).astype(jnp.float32)
        at = (h // 2) * 2 * features + 2 * DK + 2 * DV + (h % 2) * DV
        gate = arrived[:, at : at + DV].astype(jnp.float32)
        scale = lax.rsqrt(jnp.mean(core * core, axis=-1, keepdims=True) + 1e-06)
        normed = core * scale * gain[...]
        gated[:, h * DV : (h + 1) * DV] = (normed * jax.nn.silu(gate)).astype(jnp.bfloat16)
    kept = out.shape[0]

    def tokens_of(owner):
        return gated.at[pl.ds(pl.multiple_of(owner * kept, kept), kept), :]

    fourth = []
    for k in range(1, groups):
        peer = lax.rem(group + k, groups)
        fourth.append(
            send(tokens_of(peer), landed.at[group], send_d.at[k], recv_d.at[k], peer, "head")
        )
    landed[group] = tokens_of(group)[...]
    for copy in fourth:
        copy.wait()
    for g in range(groups):
        out[:, g * heads * DV : (g + 1) * heads * DV] = landed[g]


def carried(pieces, maps, reads, adds, arrived, gain):
    blocks, heads = reads.shape[:2]
    seq_len = arrived.shape[0]
    groups = lax.axis_size("head")
    width = pieces.shape[1] - DK
    piece = (ROW, DK + width, DK)
    half = (ROW, width, DK)
    full = (heads, seq_len, DK)
    vmem = pl.BlockSpec(memory_space=pltpu.VMEM)
    return pl.pallas_call(
        carry_kernel,
        out_shape=jax.ShapeDtypeStruct((seq_len // groups, groups * heads * DV), jnp.bfloat16),
        in_specs=[vmem] * 6,
        out_specs=vmem,
        scratch_shapes=[
            pltpu.VMEM(piece, jnp.float32),
            pltpu.VMEM(piece, jnp.float32),
            pltpu.VMEM(piece[1:], jnp.float32),
            pltpu.VMEM(piece, jnp.float32),
            pltpu.VMEM(half, jnp.float32),
            pltpu.VMEM(half, jnp.float32),
            pltpu.VMEM(full, jnp.float32),
            pltpu.VMEM(full, jnp.float32),
            pltpu.VMEM((seq_len, heads * DV), jnp.bfloat16),
            pltpu.VMEM((groups, seq_len // groups, heads * DV), jnp.bfloat16),
        ]
        + [pltpu.SemaphoreType.DMA((ROW,))] * 6
        + [pltpu.SemaphoreType.DMA((groups,))] * 2,
        compiler_params=pltpu.CompilerParams(collective_id=0, has_side_effects=True),
    )(pieces, maps, reads, adds, arrived, gain)


def body(projected, gate_logits, conv_weight, decay_log, step_bias, norm_gain):
    ratio = HV // KEY_HEAD_COUNT
    channels = (2 + ratio) * DK
    features = channels + ratio * DV
    logits = lax.all_to_all(gate_logits, "head", split_axis=1, concat_axis=0, tiled=True)
    arrived = lax.all_to_all(projected, "head", split_axis=1, concat_axis=0, tiled=True)
    seq_len = arrived.shape[0]
    local_keys = arrived.shape[1] // features
    heads = local_keys * ratio
    blocks = seq_len // SPAN
    logits = logits.astype(jnp.float32).reshape(seq_len, local_keys, 2, ratio)
    step_size = jax.nn.sigmoid(logits[:, :, 0].reshape(seq_len, heads))
    decays = -jnp.exp(decay_log) * jax.nn.softplus(
        logits[:, :, 1].reshape(seq_len, heads) + step_bias
    )
    sums = jnp.cumsum(decays.reshape(blocks, SPAN, heads), axis=1).transpose(0, 2, 1)
    steps = step_size.reshape(blocks, SPAN, heads).transpose(0, 2, 1)
    columns = jnp.stack([sums, steps], axis=-1)
    tail = arrived[seq_len - CONV + 1 :].reshape(CONV - 1, local_keys, features)[:, :, :channels]
    edge = passed_along(tail.reshape(CONV - 1, local_keys * channels), "ctx", 1)
    edge = jnp.concatenate([jnp.zeros((8 - CONV + 1, edge.shape[1]), edge.dtype), edge])
    pieces, maps, reads, adds = local_terms(
        arrived, edge, conv_weight.astype(jnp.float32), columns, sums[:, :, None, :]
    )
    return carried(pieces, maps, reads, adds, arrived, norm_gain.reshape(1, DV))


def solution(mesh):
    return jax.shard_map(
        body,
        mesh=mesh,
        in_specs=(
            P(("ctx", "head"), None),
            P(("ctx", "head"), None),
            P(None, "head"),
            P("head"),
            P("head"),
            P(),
        ),
        out_specs=P(("ctx", "head"), None),
        check_vma=False,
    )
```
